32 devices in a mesh: groups: 2 (over x), segment: 4 (over y, core), head: 4 (over z).
Axes of the slice: x: 2, y: 2, z: 4, core: 2. Of those that a mesh axis runs over, the one named last changes fastest.
Arguments:
- token_ids: int32 [6, 256], P('groups'), parts along dimension 0, may hold values from 0 to 18991, as said below
- embed_table: bfloat16 [18992, 256], P(('segment', 'head')), may hold values from -6 to 6
- arriving: bfloat16 [8, 256, 256], P(('groups', 'segment')), parts along dimension 0, may hold values from -16 to 16
- returning: bfloat16 [8, 256, 256], P(('groups', 'segment')), parts along dimension 0, may hold values from -6 to 6
- stashed: bfloat16 [8, 3, 256, 256], P(('groups', 'segment')), parts along dimension 0, may hold values from -16 to 16
- seed_grad: bfloat16 [6, 256, 256], P('groups'), parts along dimension 0, may hold values from -6 to 6
- expand: bfloat16 [4, 256, 2048], P('segment'), may hold values from -0.375 to 0.375
- compress: bfloat16 [4, 2048, 256], P('segment'), may hold values from -0.125 to 0.125
- norm_gain: float32 [4, 2048], P('segment'), may hold values from 0.1 to 1.9
- w_query: bfloat16 [4, 2048, 4096], P('segment', None, 'head'), may hold values from -0.125 to 0.125
- key_weight: bfloat16 [4, 2048, 512], P('segment'), may hold values from -0.125 to 0.125
- value_weight: bfloat16 [4, 2048, 512], P('segment'), may hold values from -0.125 to 0.125
- w_out: bfloat16 [4, 4096, 2048], P('segment', 'head'), may hold values from -0.09375 to 0.09375
Outputs:
- sent_forward: bfloat16 [8, 3, 256, 256], P(('groups', 'segment'), None, 'head'), parts along dimension 0
- sent_backward: bfloat16 [8, 3, 256, 256], P(('groups', 'segment'), None, 'head'), parts along dimension 0
The draws below stay inside these ranges and needn't reach their ends.
There are 2 independent parts, one for each index of `groups`. The reference program is written for one: setup_inputs(seed, part) draws one part's arguments, and reference() takes and returns one part's arrays. A program takes and returns all parts, laid end to end along the dimension named above; an argument that names none is the same for every part. Nothing has to cross between parts.
Inputs may be any that keep to these rules, and one draw needn't show every extreme that they name: `token_ids`: every aligned block of 1187 ids is named by some token.
All inputs are finite; a program needn't handle non-finite values.
Results may differ from the reference program's by a relative error of at most 0.02.
Values may be sent and summed in bfloat16 or wider, within the bound.
A program may use at most 128 MiB of HBM per device.

```python
import math
import jax
import jax.numpy as jnp
from jax import lax

MODEL_WIDTH = 2048
QUERY_HEADS = 32
KEY_VALUE_HEADS = 4
HEAD_SIZE = 128
RANK = 256
VOC_DEV = 1187
SPAN = 256
TICKS = 3
VOCAB = 18992
N_SEGMENT = 4
N_HEAD = 4


def draw_token_ids(key, part):
    token_count = TICKS * SPAN
    ranges = VOCAB // VOC_DEV
    share_rows = SPAN // N_HEAD
    drawn = jax.random.randint(jax.random.fold_in(key, 1), (token_count,), 0, VOCAB, dtype=jnp.int32)
    blocks = jnp.arange(ranges, dtype=jnp.int32)
    moved = (blocks + ranges - 1) % ranges
    share_of = moved % N_HEAD
    offset_of = moved // N_HEAD % share_rows
    tick_of = moved // SPAN
    places = (tick_of * SPAN + share_of * share_rows + offset_of).astype(jnp.int32)
    chosen = blocks * VOC_DEV + jax.random.randint(jax.random.fold_in(key, 3), (ranges,), 0, VOC_DEV, dtype=jnp.int32)
    return drawn.at[places].set(chosen).reshape(TICKS, SPAN).astype(jnp.int32)


def coefficient_rows(key, shape):
    normal_part = jax.random.normal(jax.random.fold_in(key, 21), shape, jnp.float32)
    return jnp.clip(normal_part, -16.0, 16.0).astype(jnp.bfloat16)


def draw_arriving(key, part):
    return coefficient_rows(key, (N_SEGMENT, SPAN, RANK))


def draw_stashed(key, part):
    return coefficient_rows(key, (N_SEGMENT, TICKS, SPAN, RANK))


def level_of(own_key, dims, split, least, high):
    def one(position, parts):
        steps = jax.random.uniform(jax.random.fold_in(jax.random.fold_in(own_key, 6), position), (parts,), jnp.float32, least / len(split), high / len(split))
        return jnp.repeat(jnp.exp(steps), dims[position] // parts).reshape((-1,) + (1,) * (len(dims) - position - 1))

    loudness = one(*split[0])
    for cut in split[1:]:
        loudness = loudness * one(*cut)
    return loudness


def bell_draw(key, extent, deviation, reach, cuts=(), kind=jnp.bfloat16):
    factor_of = level_of(key, extent, cuts, -0.22, 0.18) if cuts else 1.0
    values = jax.random.normal(key, extent, jnp.float32) * deviation * factor_of
    return jnp.minimum(jnp.maximum(values, -reach), reach).astype(kind)


def setup_inputs(seed: int = 0, part: int = 0) -> dict:
    streams_of = jax.random.split(jax.random.key(seed), 14)
    part_splits = jax.random.split(jax.random.fold_in(streams_of[13], part), 14)
    return {
        "token_ids": draw_token_ids(jax.random.fold_in(jax.random.fold_in(streams_of[13], part), 71), part),
        "embed_table": bell_draw(streams_of[1], (VOCAB, RANK), 1.0, 6.0, ((0, 16),)),
        "arriving": draw_arriving(jax.random.fold_in(jax.random.fold_in(streams_of[13], part), 71), part),
        "returning": bell_draw(part_splits[3], (N_SEGMENT, SPAN, RANK), 1.0, 6.0, ((0, 4),)),
        "stashed": draw_stashed(jax.random.fold_in(jax.random.fold_in(streams_of[13], part), 71), part),
        "seed_grad": bell_draw(part_splits[5], (TICKS, SPAN, RANK), 1.0, 6.0),
        "expand": bell_draw(streams_of[6], (N_SEGMENT, RANK, MODEL_WIDTH), RANK ** -0.5, 0.375, ((0, 4),)),
        "compress": bell_draw(streams_of[7], (N_SEGMENT, MODEL_WIDTH, RANK), MODEL_WIDTH ** -0.5, 0.125, ((0, 4),)),
        "norm_gain": jnp.clip(1.0 + 0.18 * jax.random.normal(streams_of[8], (N_SEGMENT, MODEL_WIDTH), jnp.float32), 0.1, 1.9),
        "w_query": bell_draw(streams_of[9], (N_SEGMENT, MODEL_WIDTH, QUERY_HEADS * HEAD_SIZE), MODEL_WIDTH ** -0.5, 0.125, ((0, 4), (2, 4))),
        "key_weight": bell_draw(streams_of[10], (N_SEGMENT, MODEL_WIDTH, KEY_VALUE_HEADS * HEAD_SIZE), MODEL_WIDTH ** -0.5, 0.125, ((0, 4),)),
        "value_weight": bell_draw(streams_of[11], (N_SEGMENT, MODEL_WIDTH, KEY_VALUE_HEADS * HEAD_SIZE), MODEL_WIDTH ** -0.5, 0.125, ((0, 4),)),
        "w_out": bell_draw(streams_of[12], (N_SEGMENT, QUERY_HEADS * HEAD_SIZE, MODEL_WIDTH), (QUERY_HEADS * HEAD_SIZE) ** -0.5, 0.09375, ((0, 4), (1, 4))),
    }


EPS = 1e-06

def rms_scale(matrix):
    return lax.rsqrt(lax.optimization_barrier(jnp.mean(matrix * matrix, axis=-1, keepdims=True)) + EPS)

def widened(matrix):
    return lax.optimization_barrier(matrix).astype(jnp.float32)

def precise(former, latter):
    return jnp.dot(former, latter, precision=lax.Precision.HIGHEST)

def precise_back(former, latter):
    return lax.dot_general(former, latter, (((1,), (1,)), ((), ())), precision=lax.Precision.HIGHEST)

def narrow_back(former, latter):
    return lax.dot_general(former, latter, (((1,), (1,)), ((), ())), preferred_element_type=jnp.float32)

def norm_back(upstream_in, grad_hat):
    scaling = rms_scale(upstream_in)
    return scaling * grad_hat - upstream_in * scaling ** 3 * lax.optimization_barrier(jnp.mean(grad_hat * upstream_in, axis=-1, keepdims=True))

def section_inputs(coeffs, expand_here, gain_here, query_here, key_here, value_here):
    row_count = coeffs.shape[0]
    hidden = jnp.dot(coeffs, expand_here, preferred_element_type=jnp.float32)
    scaling = rms_scale(hidden)
    normed = (hidden * scaling * gain_here).astype(jnp.bfloat16)
    queries = jnp.dot(normed, query_here, preferred_element_type=jnp.float32).reshape(row_count, -1, HEAD_SIZE)
    key_rows = jnp.dot(normed, key_here, preferred_element_type=jnp.float32).reshape(row_count, -1, HEAD_SIZE)
    values = jnp.dot(normed, value_here, preferred_element_type=jnp.float32).astype(jnp.bfloat16).reshape(row_count, -1, HEAD_SIZE)
    q_hat = (queries * rms_scale(queries)).astype(jnp.bfloat16)
    k_hat = (key_rows * rms_scale(key_rows)).astype(jnp.bfloat16)
    return (hidden, scaling, queries, key_rows, q_hat, k_hat, values)

def probabilities(q_hat, k_hat):
    row_count, head_count, head_width = q_hat.shape
    kv_heads = k_hat.shape[1]
    grouped = widened(q_hat).reshape(row_count, kv_heads, head_count // kv_heads, head_width)
    scores = jnp.einsum('iknd,jkd->knij', grouped, widened(k_hat)) / math.sqrt(head_width)
    causal = jnp.arange(row_count)[None, :] <= jnp.arange(row_count)[:, None]
    weights = jnp.where(causal, jnp.exp(scores), 0.0)
    return weights / lax.optimization_barrier(jnp.sum(weights, axis=-1, keepdims=True))

def section_forward(coeffs, expand_here, gain_here, query_here, key_here, value_here, out_folded, basis_folded):
    hidden, scaling, queries, key_rows, q_hat, k_hat, values = section_inputs(coeffs, expand_here, gain_here, query_here, key_here, value_here)
    weights = probabilities(q_hat, k_hat)
    low_weights = widened(weights.astype(jnp.bfloat16))
    attended = jnp.einsum('knij,jkd->iknd', low_weights, widened(values))
    attended = attended.reshape(coeffs.shape[0], -1).astype(jnp.bfloat16)
    return jnp.dot(attended, out_folded, preferred_element_type=jnp.float32) + precise(widened(coeffs), basis_folded)

def section_backward(coeffs, grads, expand_here, gain_here, query_here, key_here, value_here, out_folded, basis_folded):
    row_count = coeffs.shape[0]
    hidden, scaling, queries, key_rows, q_hat, k_hat, values = section_inputs(coeffs, expand_here, gain_here, query_here, key_here, value_here)
    weights = probabilities(q_hat, k_hat)
    head_count = queries.shape[1]
    kv_heads = key_rows.shape[1]
    query_group_size = head_count // kv_heads
    grads_wide = widened(grads)
    grad_attended = narrow_back(grads, out_folded).astype(jnp.bfloat16)
    grad_attended = widened(grad_attended).reshape(row_count, kv_heads, query_group_size, HEAD_SIZE)
    grad_weights = jnp.einsum('iknd,jkd->knij', grad_attended, widened(values))
    grad_scores = weights * (grad_weights - lax.optimization_barrier(jnp.sum(grad_weights * weights, axis=-1, keepdims=True))) / math.sqrt(HEAD_SIZE)
    grad_scores = widened(grad_scores.astype(jnp.bfloat16))
    grouped = widened(q_hat).reshape(row_count, kv_heads, query_group_size, HEAD_SIZE)
    grad_qhat = jnp.einsum('knij,jkd->iknd', grad_scores, widened(k_hat)).reshape(row_count, head_count, HEAD_SIZE)
    grad_khat = jnp.einsum('knij,iknd->jkd', grad_scores, grouped)
    low_weights = widened(weights.astype(jnp.bfloat16))
    grad_values = jnp.einsum('knij,iknd->jkd', low_weights, grad_attended).reshape(row_count, -1).astype(jnp.bfloat16)
    grad_queries = norm_back(queries, grad_qhat).reshape(row_count, -1).astype(jnp.bfloat16)
    grad_keys = norm_back(key_rows, grad_khat).reshape(row_count, -1).astype(jnp.bfloat16)
    grad_normed = narrow_back(grad_queries, query_here) + narrow_back(grad_keys, key_here) + narrow_back(grad_values, value_here)
    weighted = grad_normed * gain_here
    grad_hidden = scaling * weighted - hidden * scaling ** 3 * lax.optimization_barrier(jnp.mean(weighted * hidden, axis=-1, keepdims=True))
    grad_hidden = grad_hidden.astype(jnp.bfloat16)
    return narrow_back(grad_hidden, expand_here) + precise_back(grads_wide, basis_folded)

def reference(token_ids, embed_table, arriving, returning, stashed, seed_grad, expand, compress, norm_gain, w_query, key_weight, value_weight, w_out):
    segment_count = arriving.shape[0]
    last_segment = segment_count - 1
    embedded = embed_table[token_ids]
    folded = []
    for segment_index in range(segment_count):
        basis_folded = jnp.dot(expand[segment_index], compress[segment_index], preferred_element_type=jnp.float32)
        out_folded = jnp.dot(w_out[segment_index], compress[segment_index], preferred_element_type=jnp.float32).astype(jnp.bfloat16)
        folded.append((basis_folded, out_folded))
    history = []
    forward_sent = []
    backward_sent = []
    for tick_index in range(TICKS):
        forward_in = []
        backward_in = []
        for segment_index in range(segment_count):
            if segment_index == 0:
                forward_in.append(embedded[tick_index])
            elif tick_index == 0:
                forward_in.append(arriving[segment_index])
            else:
                forward_in.append(forward_sent[tick_index - 1][segment_index - 1])
            if segment_index == last_segment:
                backward_in.append(seed_grad[tick_index])
            elif tick_index == 0:
                backward_in.append(returning[segment_index])
            else:
                backward_in.append(backward_sent[tick_index - 1][segment_index + 1])
        history.append(forward_in)
        forward_out = []
        backward_out = []
        for segment_index in range(segment_count):
            basis_folded, out_folded = folded[segment_index]
            weights_here = (expand[segment_index], norm_gain[segment_index], w_query[segment_index], key_weight[segment_index], value_weight[segment_index])
            forward_out.append(section_forward(forward_in[segment_index], *weights_here, out_folded, basis_folded).astype(jnp.bfloat16))
            source = tick_index - 2 * (last_segment - segment_index)
            if source >= 0:
                replay = history[source][segment_index]
            else:
                replay = stashed[segment_index, tick_index]
            backward_out.append(section_backward(replay, backward_in[segment_index], *weights_here, out_folded, basis_folded).astype(jnp.bfloat16))
        forward_sent.append(forward_out)
        backward_sent.append(backward_out)
    sent_forward = jnp.stack([jnp.stack(entries) for entries in forward_sent], axis=1)
    sent_backward = jnp.stack([jnp.stack(entries) for entries in backward_sent], axis=1)
    return (sent_forward, sent_backward)
```

```python
import functools
import math

import jax
import jax.numpy as jnp
from jax import lax
from jax.experimental import pallas as pl
from jax.experimental.pallas import tpu as pltpu
from jax.sharding import PartitionSpec as P

QUERY_HEADS = 32
KEY_VALUE_HEADS = 4
HEAD_SIZE = 128
EPS = 1e-06
MESH = pl.DeviceIdType.MESH
F32 = jnp.float32
BF16 = jnp.bfloat16


def mm(former, latter):
    return jnp.dot(former, latter, preferred_element_type=F32)


def mm_back(former, latter):
    return lax.dot_general(former, latter, (((1,), (1,)), ((), ())), preferred_element_type=F32)


def mm_down(former, latter):
    return lax.dot_general(former, latter, (((0,), (0,)), ((), ())), preferred_element_type=F32)


def halves(matrix):
    upper = matrix.astype(BF16)
    return upper, (matrix - upper.astype(F32)).astype(BF16)


def relay(
    ids_ref,
    table_ref,
    gain_ref,
    arriving,
    returning,
    stashed,
    seed_grad,
    expand,
    compress,
    w_query,
    key_weight,
    value_weight,
    w_out,
    fwd_ref,
    bwd_ref,
    expand_v,
    compress_v,
    query_v,
    kv_v,
    out_v,
    qkv_f,
    out_f,
    gram,
    basis,
    coef,
    grad_in,
    mixed_s,
    scale_s,
    qhat_s,
    rq_s,
    khat_s,
    rk_s,
    vals_s,
    probs_s,
    wide_s,
    gkv_acc,
    gcat,
    part,
    own,
    rs_in,
    e_part,
    e_in1,
    e_sum,
    e_in2,
    ld_sem,
    rs_send,
    rs_recv,
    ag_send,
    ag_recv,
    e1_send,
    e1_recv,
    e2_send,
    e2_recv,
    e3_send,
    e3_recv,
    *,
    segments,
    head_groups,
    table_rows,
):
    seg = lax.axis_index("segment")
    me = lax.axis_index("head")
    last = segments - 1
    ticks, span = ids_ref.shape
    share = span // head_groups
    width = expand_v.shape[1]
    heads = query_v.shape[1] // HEAD_SIZE
    nq = heads * HEAD_SIZE
    kv_group = QUERY_HEADS // KEY_VALUE_HEADS
    first_kv = me * heads // kv_group
    kv_cols = pl.ds(pl.multiple_of(first_kv * HEAD_SIZE, HEAD_SIZE), HEAD_SIZE)
    inv = 1.0 / math.sqrt(HEAD_SIZE)
    own_rows = pl.ds(pl.multiple_of(me * share, share), share)

    def rows_of(head):
        return pl.ds(pl.multiple_of(head * share, share), share)

    def peer(off):
        return lax.rem(me + off, head_groups)

    qchunk = min(256, nq)
    pieces = nq // qchunk
    loads = [
        (expand.at[0], expand_v),
        *[
            (
                w_query.at[0, :, i * qchunk : (i + 1) * qchunk],
                query_v.at[:, i * qchunk : (i + 1) * qchunk],
            )
            for i in range(pieces)
        ],
        (key_weight.at[0, :, kv_cols], kv_v.at[:, :HEAD_SIZE]),
        (value_weight.at[0, :, kv_cols], kv_v.at[:, HEAD_SIZE:]),
        (stashed.at[0], coef.at[ticks : 2 * ticks]),
        (compress.at[0], compress_v),
        *[
            (
                w_out.at[0, i * qchunk : (i + 1) * qchunk, :],
                out_v.at[i * qchunk : (i + 1) * qchunk, :],
            )
            for i in range(pieces)
        ],
    ]
    loads = [
        pltpu.make_async_copy(src, dst, ld_sem.at[i]) for i, (src, dst) in enumerate(loads)
    ]
    fixed = len(loads)
    arr_copy = pltpu.make_async_copy(arriving.at[0], coef.at[0], ld_sem.at[fixed])
    ret_copy = pltpu.make_async_copy(returning.at[0], grad_in.at[0], ld_sem.at[fixed + 1])
    seed_copy = pltpu.make_async_copy(seed_grad, grad_in, ld_sem.at[fixed + 1])
    for one in loads:
        one.start()

    @pl.when(seg > 0)
    def _():
        arr_copy.start()

    @pl.when(seg < last)
    def _():
        ret_copy.start()

    @pl.when(seg == last)
    def _():
        seed_copy.start()

    barrier = pltpu.get_barrier_semaphore()
    total = segments * head_groups
    mine = seg * head_groups + me
    for off in range(1, total):
        other = lax.rem(mine + off, total)
        pl.semaphore_signal(
            barrier,
            inc=1,
            device_id={
                "segment": other // head_groups,
                "head": lax.rem(other, head_groups),
            },
            device_id_type=MESH,
        )

    base = mine * table_rows
    for t in range(ticks):
        wanted = ids_ref[t : t + 1, :] - base
        places = lax.broadcasted_iota(jnp.int32, (table_ref.shape[0], span), 0)
        hot = jnp.where(places == wanted, 1.0, 0.0).astype(BF16)
        e_part[t] = mm_down(hot, table_ref[...]).astype(BF16)
    pl.semaphore_wait(barrier, total - 1)

    def e1_copy(t, slot):
        return pltpu.make_async_remote_copy(
            src_ref=e_part.at[t],
            dst_ref=e_in1.at[slot, t],
            send_sem=e1_send.at[t],
            recv_sem=e1_recv.at[slot, t],
            device_id={"segment": 0, "head": me},
            device_id_type=MESH,
        )

    @pl.when(seg > 0)
    def _():
        for t in range(ticks):
            e1_copy(t, seg).start()

    def e2_copy(t, off):
        return pltpu.make_async_remote_copy(
            src_ref=e_sum.at[t, rows_of(peer(off))],
            dst_ref=e_in2.at[t, off],
            send_sem=e2_send.at[t, off],
            recv_sem=e2_recv.at[t, off],
            device_id={"segment": seg, "head": peer(off)},
            device_id_type=MESH,
        )

    def e3_copy(t, off):
        return pltpu.make_async_remote_copy(
            src_ref=coef.at[t, own_rows],
            dst_ref=coef.at[t, own_rows],
            send_sem=e3_send.at[t, off],
            recv_sem=e3_recv.at[t, off],
            device_id={"segment": seg, "head": peer(off)},
            device_id_type=MESH,
        )

    def embed_sum(t):
        total_rows = e_part[t].astype(F32)
        for other in range(1, segments):
            e1_copy(t, other).wait_recv()
            total_rows = total_rows + e_in1[other, t].astype(F32)
        e_sum[t] = total_rows.astype(BF16)
        for off in range(1, head_groups):
            e2_copy(t, off).start()

    def embed_share(t):
        rows = e_sum[t, own_rows].astype(F32)
        for off in range(1, head_groups):
            e2_copy(t, off).wait_recv()
            rows = rows + e_in2[t, off].astype(F32)
        coef[t, own_rows] = rows.astype(BF16)
        for off in range(1, head_groups):
            e3_copy(t, off).start()

    def rs_copy(way, t, off):
        return pltpu.make_async_remote_copy(
            src_ref=part.at[way, t, rows_of(peer(off))],
            dst_ref=rs_in.at[way, t, off],
            send_sem=rs_send.at[way, t, off],
            recv_sem=rs_recv.at[way, t, off],
            device_id={"segment": seg, "head": peer(off)},
            device_id_type=MESH,
        )

    def ag_copy(way, t, from_head, to_head):
        target = coef if way == 0 else grad_in
        return pltpu.make_async_remote_copy(
            src_ref=own.at[way, t],
            dst_ref=target.at[t + 1, rows_of(from_head)],
            send_sem=ag_send.at[way, t, to_head],
            recv_sem=ag_recv.at[way, t, from_head],
            device_id={"segment": seg + (1 if way == 0 else -1), "head": to_head},
            device_id_type=MESH,
        )

    def summed(way, t):
        rows = part[way, t, own_rows].astype(F32)
        for off in range(1, head_groups):
            rs_copy(way, t, off).wait_recv()
            rows = rows + rs_in[way, t, off].astype(F32)
        return rows

    def pass_on(way, t):
        for to_head in range(head_groups):
            ag_copy(way, t, me, to_head).start()

    def replay_index(t):
        source = t - 2 * (last - seg)
        return jnp.where(source >= 0, source, ticks + t)

    def state_slot(t):
        return jnp.where(seg == last, 2 + lax.rem(t, 2), lax.rem(t, 2))

    causal = lax.broadcasted_iota(jnp.int32, (span, span), 1) <= lax.broadcasted_iota(
        jnp.int32, (span, span), 0
    )

    def section(index, slot, with_out):
        c = coef[index]
        wide = c.astype(F32)
        mixed = mm(c, gram[0]) + mm(c, gram[1])
        scaling = lax.rsqrt(jnp.sum(mixed * wide, axis=-1, keepdims=True) / width + EPS)
        mixed_s[slot] = mixed
        scale_s[slot] = scaling
        kv = mm(c, qkv_f[:, nq:]) * scaling
        keys = kv[:, :HEAD_SIZE]
        rk = lax.rsqrt(jnp.mean(keys * keys, axis=-1, keepdims=True) + EPS)
        khat = (keys * rk).astype(BF16)
        values = kv[:, HEAD_SIZE:].astype(BF16)
        khat_s[slot] = khat
        rk_s[slot] = rk
        vals_s[slot] = values

        def pair(i, carry):
            cols = pl.ds(pl.multiple_of(i * 2 * HEAD_SIZE, 2 * HEAD_SIZE), 2 * HEAD_SIZE)
            both = mm(coef[index], qkv_f[:, cols]) * scale_s[slot]
            outs = []
            for e in range(2):
                h = 2 * i + e
                q = both[:, e * HEAD_SIZE : (e + 1) * HEAD_SIZE]
                rq = lax.rsqrt(jnp.mean(q * q, axis=-1, keepdims=True) + EPS)
                qhat = (q * rq).astype(BF16)
                qhat_s[slot, h] = qhat
                rq_s[slot, h] = rq
                raw = mm_back(qhat, khat_s[slot]) * inv
                weights = jnp.where(causal, jnp.exp(raw), 0.0)
                low = (weights * (1.0 / jnp.sum(weights, axis=-1, keepdims=True))).astype(BF16)
                probs_s[slot, h] = low
                if with_out:
                    outs.append(mm(low, vals_s[slot]).astype(BF16))
            if with_out:
                wide_s[:, cols] = jnp.concatenate(outs, axis=1)
            return carry

        lax.fori_loop(0, heads // 2, pair, 0)

    def forward(t):
        section(t, 2 + lax.rem(t, 2), True)
        part[0, t] = mm(wide_s[...], out_f[...]).astype(BF16)
        for off in range(1, head_groups):
            rs_copy(0, t, off).start()

    def finish_forward(t):
        c = coef[t, own_rows]
        rows = summed(0, t) + (mm(c, basis[0]) + mm(c, basis[1]))
        rows = rows.astype(BF16)
        own[0, t] = rows
        fwd_ref[0, t] = rows

        @pl.when(jnp.logical_and(seg < last, t + 1 < ticks))
        def _():
            pass_on(0, t)

    def backward(t):
        slot = state_slot(t)
        wide_s[...] = mm_back(grad_in[t], out_f[...]).astype(BF16)
        gkv_acc[...] = jnp.zeros_like(gkv_acc)

        def pair(i, carry):
            cols = pl.ds(pl.multiple_of(i * 2 * HEAD_SIZE, 2 * HEAD_SIZE), 2 * HEAD_SIZE)
            both = wide_s[:, cols]
            outs = []
            for e in range(2):
                h = 2 * i + e
                ga = both[:, e * HEAD_SIZE : (e + 1) * HEAD_SIZE]
                low = probs_s[slot, h]
                probs = low.astype(F32)
                gp = mm_back(ga, vals_s[slot])
                inner = jnp.sum(gp * probs, axis=-1, keepdims=True)
                gs = (probs * ((gp - inner) * inv)).astype(BF16)
                qhat = qhat_s[slot, h]
                gqh = mm(gs, khat_s[slot])
                gkv_acc[0] += mm_down(gs, qhat)
                gkv_acc[1] += mm_down(low, ga)
                qw = qhat.astype(F32)
                along = jnp.mean(gqh * qw, axis=-1, keepdims=True)
                outs.append((rq_s[slot, h] * (gqh - qw * along)).astype(BF16))
            gcat[:, cols] = jnp.concatenate(outs, axis=1)
            return carry

        lax.fori_loop(0, heads // 2, pair, 0)
        gkh = gkv_acc[0]
        kw = khat_s[slot].astype(F32)
        along = jnp.mean(gkh * kw, axis=-1, keepdims=True)
        gcat[:, nq : nq + HEAD_SIZE] = (rk_s[slot] * (gkh - kw * along)).astype(BF16)
        gcat[:, nq + HEAD_SIZE :] = gkv_acc[1].astype(BF16)
        part[1, t] = mm_back(gcat[...], qkv_f[...]).astype(BF16)
        for off in range(1, head_groups):
            rs_copy(1, t, off).start()

    def finish_backward(t):
        slot = state_slot(t)
        c = coef[replay_index(t), own_rows].astype(F32)
        g = grad_in[t, own_rows]
        scaling = scale_s[slot, own_rows]
        pulled = summed(1, t)
        along = jnp.sum(pulled * c, axis=-1, keepdims=True) / width
        direct = mm_back(g, basis[0]) + mm_back(g, basis[1])
        rows = (
            scaling * pulled
            - mixed_s[slot, own_rows] * (scaling * scaling * scaling * along)
            + direct
        ).astype(BF16)
        own[1, t] = rows
        bwd_ref[0, t] = rows

        @pl.when(jnp.logical_and(seg > 0, t + 1 < ticks))
        def _():
            pass_on(1, t)

    loads[0].wait()
    gained = (expand_v[...].astype(F32) * gain_ref[...]).astype(BF16)
    up, low = halves(mm_back(expand_v[...], expand_v[...]))
    gram[0] = up
    gram[1] = low
    for i in range(pieces):
        loads[1 + i].wait()
        cols = slice(i * qchunk, (i + 1) * qchunk)
        qkv_f[:, cols] = mm(gained, query_v[:, cols]).astype(BF16)
    loads[1 + pieces].wait()
    loads[2 + pieces].wait()
    qkv_f[:, nq:] = mm(gained, kv_v[...]).astype(BF16)
    loads[3 + pieces].wait()
    loads[4 + pieces].wait()
    up, low = halves(mm(expand_v[...], compress_v[...]))
    basis[0] = up
    basis[1] = low
    for i in range(pieces):
        loads[5 + pieces + i].wait()
        rows = slice(i * qchunk, (i + 1) * qchunk)
        out_f[rows] = mm(out_v[rows, :], compress_v[...]).astype(BF16)

    @pl.when(seg > 0)
    def _():
        arr_copy.wait()

    @pl.when(seg < last)
    def _():
        ret_copy.wait()

    @pl.when(seg == last)
    def _():
        seed_copy.wait()

    @pl.when(seg == 0)
    def _():
        embed_sum(0)

    def replay_section(t):
        section(replay_index(t), lax.rem(t, 2), False)

    @pl.when(seg < last)
    def _():
        replay_section(0)

    @pl.when(seg == 0)
    def _():
        embed_share(0)

    def tick(t, carry):
        more = t + 1 < ticks

        @pl.when(seg == 0)
        def _():
            for off in range(1, head_groups):
                theirs = lax.rem(me + head_groups - off, head_groups)
                pltpu.make_async_remote_copy(
                    src_ref=coef.at[t, rows_of(theirs)],
                    dst_ref=coef.at[t, rows_of(theirs)],
                    send_sem=e3_send.at[t, off],
                    recv_sem=e3_recv.at[t, off],
                    device_id={"segment": seg, "head": peer(off)},
                    device_id_type=MESH,
                ).wait_recv()

        @pl.when(jnp.logical_and(seg > 0, t > 0))
        def _():
            for from_head in range(head_groups):
                ag_copy(0, t - 1, from_head, from_head).wait_recv()

        forward(t)

        @pl.when(t > 0)
        def _():
            finish_backward(t - 1)

        @pl.when(jnp.logical_and(seg == 0, more))
        def _():
            embed_sum(t + 1)

        @pl.when(jnp.logical_and(seg < last, more))
        def _():
            replay_section(t + 1)

        @pl.when(jnp.logical_and(seg == 0, more))
        def _():
            embed_share(t + 1)

        finish_forward(t)

        @pl.when(jnp.logical_and(seg < last, t > 0))
        def _():
            for from_head in range(head_groups):
                ag_copy(1, t - 1, from_head, from_head).wait_recv()

        backward(t)
        return carry

    lax.fori_loop(0, ticks, tick, 0)
    finish_backward(ticks - 1)

    def drain(t, carry):
        for off in range(1, head_groups):
            rs_copy(0, t, off).wait_send()
            rs_copy(1, t, off).wait_send()

        @pl.when(seg > 0)
        def _():
            e1_copy(t, seg).wait_send()

        @pl.when(seg == 0)
        def _():
            for off in range(1, head_groups):
                e2_copy(t, off).wait_send()
                e3_copy(t, off).wait_send()

        @pl.when(jnp.logical_and(seg < last, t + 1 < ticks))
        def _():
            for to_head in range(head_groups):
                ag_copy(0, t, me, to_head).wait_send()

        @pl.when(jnp.logical_and(seg > 0, t + 1 < ticks))
        def _():
            for to_head in range(head_groups):
                ag_copy(1, t, me, to_head).wait_send()

        return carry

    lax.fori_loop(0, ticks, drain, 0)


def shards(
    token_ids,
    embed_table,
    arriving,
    returning,
    stashed,
    seed_grad,
    expand,
    compress,
    norm_gain,
    w_query,
    key_weight,
    value_weight,
    w_out,
):
    segments = lax.axis_size("segment")
    head_groups = lax.axis_size("head")
    ticks, span = token_ids.shape
    rank = embed_table.shape[1]
    width = expand.shape[2]
    nq = w_query.shape[2]
    heads = nq // HEAD_SIZE
    share = span // head_groups
    table_rows = embed_table.shape[0]
    padded = -(-table_rows // 128) * 128
    table = jnp.pad(embed_table, ((0, padded - table_rows), (0, 0)))
    vmem = pl.BlockSpec(memory_space=pltpu.VMEM)
    hbm = pl.BlockSpec(memory_space=pl.ANY)
    V = pltpu.VMEM
    D = pltpu.SemaphoreType.DMA
    pieces = nq // min(256, nq)
    all_cols = nq + 2 * HEAD_SIZE
    slots = 4
    out = jax.ShapeDtypeStruct((1, ticks, share, rank), BF16)
    return pl.pallas_call(
        functools.partial(
            relay, segments=segments, head_groups=head_groups, table_rows=table_rows
        ),
        out_shape=(out, out),
        in_specs=[vmem] * 3 + [hbm] * 10,
        out_specs=(vmem, vmem),
        scratch_shapes=[
            V((rank, width), BF16),
            V((width, rank), BF16),
            V((width, nq), BF16),
            V((width, 2 * HEAD_SIZE), BF16),
            V((nq, width), BF16),
            V((rank, all_cols), BF16),
            V((nq, rank), BF16),
            V((2, rank, rank), BF16),
            V((2, rank, rank), BF16),
            V((2 * ticks, span, rank), BF16),
            V((ticks, span, rank), BF16),
            V((slots, span, rank), F32),
            V((slots, span, 1), F32),
            V((slots, heads, span, HEAD_SIZE), BF16),
            V((slots, heads, span, 1), F32),
            V((slots, span, HEAD_SIZE), BF16),
            V((slots, span, 1), F32),
            V((slots, span, HEAD_SIZE), BF16),
            V((slots, heads, span, span), BF16),
            V((span, nq), BF16),
            V((2, span, HEAD_SIZE), F32),
            V((span, all_cols), BF16),
            V((2, ticks, span, rank), BF16),
            V((2, ticks, share, rank), BF16),
            V((2, ticks, head_groups, share, rank), BF16),
            V((ticks, span, rank), BF16),
            V((segments, ticks, span, rank), BF16),
            V((ticks, span, rank), BF16),
            V((ticks, head_groups, share, rank), BF16),
            D((7 + 2 * pieces,)),
            D((2, ticks, head_groups)),
            D((2, ticks, head_groups)),
            D((2, ticks, head_groups)),
            D((2, ticks, head_groups)),
            D((ticks,)),
            D((segments, ticks)),
            D((ticks, head_groups)),
            D((ticks, head_groups)),
            D((ticks, head_groups)),
            D((ticks, head_groups)),
        ],
        compiler_params=pltpu.CompilerParams(
            collective_id=0, has_side_effects=True, vmem_limit_bytes=62 << 20
        ),
        name="relay",
    )(
        token_ids,
        table,
        norm_gain,
        arriving,
        returning,
        stashed,
        seed_grad,
        expand,
        compress,
        w_query,
        key_weight,
        value_weight,
        w_out,
    )


def solution(mesh):
    return jax.shard_map(
        shards,
        mesh=mesh,
        in_specs=(
            P("groups", None),
            P(("segment", "head"), None),
            P(("groups", "segment"), None, None),
            P(("groups", "segment"), None, None),
            P(("groups", "segment"), None, None, None),
            P("groups", None, None),
            P("segment", None, None),
            P("segment", None, None),
            P("segment", None),
            P("segment", None, "head"),
            P("segment", None, None),
            P("segment", None, None),
            P("segment", "head", None),
        ),
        out_specs=(
            P(("groups", "segment"), None, "head", None),
            P(("groups", "segment"), None, "head", None),
        ),
        check_vma=False,
    )
```

```python
import functools
import math

import jax
import jax.numpy as jnp
from jax import lax
from jax.experimental import pallas as pl
from jax.experimental.pallas import tpu as pltpu
from jax.sharding import PartitionSpec as P

QUERY_HEADS = 32
KEY_VALUE_HEADS = 4
HEAD_SIZE = 128
EPS = 1e-06
MESH = pl.DeviceIdType.MESH
F32 = jnp.float32
BF16 = jnp.bfloat16


def mm(former, latter):
    return jnp.dot(former, latter, preferred_element_type=F32)


def mm_back(former, latter):
    return lax.dot_general(former, latter, (((1,), (1,)), ((), ())), preferred_element_type=F32)


def mm_down(former, latter):
    return lax.dot_general(former, latter, (((0,), (0,)), ((), ())), preferred_element_type=F32)


def halves(matrix):
    upper = matrix.astype(BF16)
    return upper, (matrix - upper.astype(F32)).astype(BF16)


def relay(
    ids_ref,
    table_ref,
    gain_ref,
    arriving,
    returning,
    stashed,
    seed_grad,
    expand,
    compress,
    w_query,
    key_weight,
    value_weight,
    w_out,
    fwd_ref,
    bwd_ref,
    expand_v,
    compress_v,
    query_v,
    kv_v,
    out_v,
    qkv_f,
    out_f,
    gram,
    basis,
    coef,
    grad_in,
    mixed_s,
    scale_s,
    qhat_s,
    rq_s,
    khat_s,
    rk_s,
    vals_s,
    probs_s,
    wide_s,
    gkv_acc,
    gcat,
    part,
    own,
    rs_in,
    e_part,
    e_in1,
    e_sum,
    e_in2,
    tail,
    ld_sem,
    rs_send,
    rs_recv,
    ag_send,
    ag_recv,
    e1_send,
    e1_recv,
    e2_send,
    e2_recv,
    e3_send,
    e3_recv,
    *,
    segments,
    head_groups,
    table_rows,
):
    seg = lax.axis_index("segment")
    me = lax.axis_index("head")
    last = segments - 1
    ticks, span = ids_ref.shape
    share = span // head_groups
    width = expand_v.shape[1]
    heads = query_v.shape[1] // HEAD_SIZE
    nq = heads * HEAD_SIZE
    kv_group = QUERY_HEADS // KEY_VALUE_HEADS
    first_kv = me * heads // kv_group
    kv_cols = pl.ds(pl.multiple_of(first_kv * HEAD_SIZE, HEAD_SIZE), HEAD_SIZE)
    inv = 1.0 / math.sqrt(HEAD_SIZE)
    own_rows = pl.ds(pl.multiple_of(me * share, share), share)

    def rows_of(head):
        return pl.ds(pl.multiple_of(head * share, share), share)

    def peer(off):
        return lax.rem(me + off, head_groups)

    qchunk = min(256, nq)
    pieces = nq // qchunk
    loads = [
        (expand.at[0], expand_v),
        *[
            (
                w_query.at[0, :, i * qchunk : (i + 1) * qchunk],
                query_v.at[:, i * qchunk : (i + 1) * qchunk],
            )
            for i in range(pieces)
        ],
        (key_weight.at[0, :, kv_cols], kv_v.at[:, :HEAD_SIZE]),
        (value_weight.at[0, :, kv_cols], kv_v.at[:, HEAD_SIZE:]),
        (stashed.at[0], coef.at[ticks : 2 * ticks]),
        (compress.at[0], compress_v),
        *[
            (
                w_out.at[0, i * qchunk : (i + 1) * qchunk, :],
                out_v.at[i * qchunk : (i + 1) * qchunk, :],
            )
            for i in range(pieces)
        ],
    ]
    loads = [
        pltpu.make_async_copy(src, dst, ld_sem.at[i]) for i, (src, dst) in enumerate(loads)
    ]
    fixed = len(loads)
    arr_copy = pltpu.make_async_copy(arriving.at[0], coef.at[0], ld_sem.at[fixed])
    ret_copy = pltpu.make_async_copy(returning.at[0], grad_in.at[0], ld_sem.at[fixed + 1])
    seed_copy = pltpu.make_async_copy(seed_grad, grad_in, ld_sem.at[fixed + 1])
    for one in loads:
        one.start()

    @pl.when(seg > 0)
    def _():
        arr_copy.start()

    @pl.when(seg < last)
    def _():
        ret_copy.start()

    @pl.when(seg == last)
    def _():
        seed_copy.start()

    barrier = pltpu.get_barrier_semaphore()
    total = segments * head_groups
    mine = seg * head_groups + me
    for off in range(1, total):
        other = lax.rem(mine + off, total)
        pl.semaphore_signal(
            barrier,
            inc=1,
            device_id={
                "segment": other // head_groups,
                "head": lax.rem(other, head_groups),
            },
            device_id_type=MESH,
        )

    base = mine * table_rows
    main = table_rows // HEAD_SIZE * HEAD_SIZE
    rest = table_rows - main
    even = rest // 16 * 16
    tail[...] = jnp.zeros_like(tail)
    if even:
        tail[:even] = table_ref[main : main + even, :]
    if rest > even:
        tail[even:rest] = table_ref[main + even : table_rows, :]

    def pick(t):
        wanted = ids_ref[t : t + 1, :] - base

        def hot(start, count):
            places = lax.broadcasted_iota(jnp.int32, (count, span), 0) + start
            return jnp.where(places == wanted, 1.0, 0.0).astype(BF16)

        rows = mm_down(hot(main, HEAD_SIZE), tail[...])
        if main:
            rows = rows + mm_down(hot(0, main), table_ref[:main, :])
        e_part[t] = rows.astype(BF16)

    pick(0)
    pl.semaphore_wait(barrier, total - 1)

    def e1_copy(t, slot):
        return pltpu.make_async_remote_copy(
            src_ref=e_part.at[t],
            dst_ref=e_in1.at[slot, t],
            send_sem=e1_send.at[t],
            recv_sem=e1_recv.at[slot, t],
            device_id={"segment": 0, "head": me},
            device_id_type=MESH,
        )

    @pl.when(seg > 0)
    def _():
        e1_copy(0, seg).start()

    for t in range(1, ticks):
        pick(t)

    def e2_copy(t, off):
        return pltpu.make_async_remote_copy(
            src_ref=e_sum.at[t, rows_of(peer(off))],
            dst_ref=e_in2.at[t, off],
            send_sem=e2_send.at[t, off],
            recv_sem=e2_recv.at[t, off],
            device_id={"segment": seg, "head": peer(off)},
            device_id_type=MESH,
        )

    def e3_copy(t, off):
        return pltpu.make_async_remote_copy(
            src_ref=coef.at[t, own_rows],
            dst_ref=coef.at[t, own_rows],
            send_sem=e3_send.at[t, off],
            recv_sem=e3_recv.at[t, off],
            device_id={"segment": seg, "head": peer(off)},
            device_id_type=MESH,
        )

    def embed_sum(t):
        total_rows = e_part[t].astype(F32)
        for other in range(1, segments):
            e1_copy(t, other).wait_recv()
            total_rows = total_rows + e_in1[other, t].astype(F32)
        e_sum[t] = total_rows.astype(BF16)
        for off in range(1, head_groups):
            e2_copy(t, off).start()

    def embed_share(t):
        rows = e_sum[t, own_rows].astype(F32)
        for off in range(1, head_groups):
            e2_copy(t, off).wait_recv()
            rows = rows + e_in2[t, off].astype(F32)
        coef[t, own_rows] = rows.astype(BF16)
        for off in range(1, head_groups):
            e3_copy(t, off).start()

    def rs_copy(way, t, off):
        return pltpu.make_async_remote_copy(
            src_ref=part.at[way, t, rows_of(peer(off))],
            dst_ref=rs_in.at[way, t, off],
            send_sem=rs_send.at[way, t, off],
            recv_sem=rs_recv.at[way, t, off],
            device_id={"segment": seg, "head": peer(off)},
            device_id_type=MESH,
        )

    def ag_copy(way, t, from_head, to_head):
        target = coef if way == 0 else grad_in
        return pltpu.make_async_remote_copy(
            src_ref=own.at[way, t],
            dst_ref=target.at[t + 1, rows_of(from_head)],
            send_sem=ag_send.at[way, t, to_head],
            recv_sem=ag_recv.at[way, t, from_head],
            device_id={"segment": seg + (1 if way == 0 else -1), "head": to_head},
            device_id_type=MESH,
        )

    def summed(way, t):
        rows = part[way, t, own_rows].astype(F32)
        for off in range(1, head_groups):
            rs_copy(way, t, off).wait_recv()
            rows = rows + rs_in[way, t, off].astype(F32)
        return rows

    def pass_on(way, t):
        for to_head in range(head_groups):
            ag_copy(way, t, me, to_head).start()

    def replay_index(t):
        source = t - 2 * (last - seg)
        return jnp.where(source >= 0, source, ticks + t)

    def state_slot(t):
        return jnp.where(seg == last, 2 + lax.rem(t, 2), lax.rem(t, 2))

    half = span // 2

    def pair_cols(i):
        return pl.ds(pl.multiple_of(i * 2 * HEAD_SIZE, 2 * HEAD_SIZE), 2 * HEAD_SIZE)

    causal = []
    for rb in range(2):
        shape = (half, (rb + 1) * half)
        row = lax.broadcasted_iota(jnp.int32, shape, 0) + rb * half
        row = jnp.concatenate([row, row], axis=0)
        causal.append(lax.broadcasted_iota(jnp.int32, row.shape, 1) <= row)

    def section(index, slot, with_out):
        c = coef[index]
        wide = c.astype(F32)
        mixed = mm(c, gram[0]) + mm(c, gram[1])
        scaling = lax.rsqrt(jnp.sum(mixed * wide, axis=-1, keepdims=True) / width + EPS)
        mixed_s[slot] = mixed
        scale_s[slot] = scaling
        kv = mm(c, qkv_f[:, nq:]) * scaling
        keys = kv[:, :HEAD_SIZE]
        rk = lax.rsqrt(jnp.mean(keys * keys, axis=-1, keepdims=True) + EPS)
        khat = (keys * rk).astype(BF16)
        values = kv[:, HEAD_SIZE:].astype(BF16)
        khat_s[slot] = khat
        rk_s[slot] = rk
        vals_s[slot] = values

        def pair(i, carry):
            cols = pair_cols(i)
            both = mm(coef[index], qkv_f[:, cols]) * scale_s[slot]
            hats = []
            scales = []
            for e in range(2):
                q = both[:, e * HEAD_SIZE : (e + 1) * HEAD_SIZE]
                rq = lax.rsqrt(jnp.mean(q * q, axis=-1, keepdims=True) + EPS)
                hats.append((q * rq).astype(BF16))
                scales.append(rq)
            for rb in range(2):
                rows = slice(rb * half, (rb + 1) * half)
                known = (rb + 1) * half
                qq = jnp.concatenate([x[rows] for x in hats], axis=0)
                qhat_s[slot, i, rb] = qq
                rq_s[slot, i, rb] = jnp.concatenate([x[rows] for x in scales], axis=0)
                raw = mm_back(qq, khat_s[slot, :known]) * inv
                weights = jnp.where(causal[rb], jnp.exp(raw), 0.0)
                low = (weights * (1.0 / jnp.sum(weights, axis=-1, keepdims=True))).astype(BF16)
                probs_s[slot, i, rb, :, :known] = low
                if with_out:
                    att = mm(low, vals_s[slot, :known]).astype(BF16)
                    wide_s[rows, cols] = jnp.concatenate([att[:half], att[half:]], axis=1)
            return carry

        lax.fori_loop(0, heads // 2, pair, 0)

    def forward(t):
        section(t, 2 + lax.rem(t, 2), True)
        part[0, t] = mm(wide_s[...], out_f[...]).astype(BF16)
        for off in range(1, head_groups):
            rs_copy(0, t, off).start()

    def finish_forward(t):
        c = coef[t, own_rows]
        rows = summed(0, t) + (mm(c, basis[0]) + mm(c, basis[1]))
        rows = rows.astype(BF16)
        own[0, t] = rows
        fwd_ref[0, t] = rows

        @pl.when(jnp.logical_and(seg < last, t + 1 < ticks))
        def _():
            pass_on(0, t)

    def backward(t):
        slot = state_slot(t)
        wide_s[...] = mm_back(grad_in[t], out_f[...]).astype(BF16)
        gkv_acc[...] = jnp.zeros_like(gkv_acc)

        def pair(i, carry):
            cols = pair_cols(i)
            for rb in range(2):
                rows = slice(rb * half, (rb + 1) * half)
                known = (rb + 1) * half
                both = wide_s[rows, cols]
                ga = jnp.concatenate([both[:, :HEAD_SIZE], both[:, HEAD_SIZE:]], axis=0)
                low = probs_s[slot, i, rb, :, :known]
                probs = low.astype(F32)
                gp = mm_back(ga, vals_s[slot, :known])
                inner = jnp.sum(gp * probs, axis=-1, keepdims=True)
                gs = (probs * ((gp - inner) * inv)).astype(BF16)
                qhat = qhat_s[slot, i, rb]
                gqh = mm(gs, khat_s[slot, :known])
                gkv_acc[0, :known] += mm_down(gs, qhat)
                gkv_acc[1, :known] += mm_down(low, ga)
                qw = qhat.astype(F32)
                along = jnp.mean(gqh * qw, axis=-1, keepdims=True)
                gq = (rq_s[slot, i, rb] * (gqh - qw * along)).astype(BF16)
                gcat[rows, cols] = jnp.concatenate([gq[:half], gq[half:]], axis=1)
            return carry

        lax.fori_loop(0, heads // 2, pair, 0)
        gkh = gkv_acc[0]
        kw = khat_s[slot].astype(F32)
        along = jnp.mean(gkh * kw, axis=-1, keepdims=True)
        gcat[:, nq : nq + HEAD_SIZE] = (rk_s[slot] * (gkh - kw * along)).astype(BF16)
        gcat[:, nq + HEAD_SIZE :] = gkv_acc[1].astype(BF16)
        part[1, t] = mm_back(gcat[...], qkv_f[...]).astype(BF16)
        for off in range(1, head_groups):
            rs_copy(1, t, off).start()

    def finish_backward(t):
        slot = state_slot(t)
        c = coef[replay_index(t), own_rows].astype(F32)
        g = grad_in[t, own_rows]
        scaling = scale_s[slot, own_rows]
        pulled = summed(1, t)
        along = jnp.sum(pulled * c, axis=-1, keepdims=True) / width
        direct = mm_back(g, basis[0]) + mm_back(g, basis[1])
        rows = (
            scaling * pulled
            - mixed_s[slot, own_rows] * (scaling * scaling * scaling * along)
            + direct
        ).astype(BF16)
        own[1, t] = rows
        bwd_ref[0, t] = rows

        @pl.when(jnp.logical_and(seg > 0, t + 1 < ticks))
        def _():
            pass_on(1, t)

    loads[0].wait()
    gained = (expand_v[...].astype(F32) * gain_ref[...]).astype(BF16)
    up, low = halves(mm_back(expand_v[...], expand_v[...]))
    gram[0] = up
    gram[1] = low
    for i in range(pieces):
        loads[1 + i].wait()
        cols = slice(i * qchunk, (i + 1) * qchunk)
        qkv_f[:, cols] = mm(gained, query_v[:, cols]).astype(BF16)
    loads[1 + pieces].wait()
    loads[2 + pieces].wait()
    qkv_f[:, nq:] = mm(gained, kv_v[...]).astype(BF16)

    @pl.when(seg == 0)
    def _():
        embed_sum(0)

    loads[3 + pieces].wait()
    loads[4 + pieces].wait()
    up, low = halves(mm(expand_v[...], compress_v[...]))
    basis[0] = up
    basis[1] = low
    for i in range(pieces):
        loads[5 + pieces + i].wait()
        rows = slice(i * qchunk, (i + 1) * qchunk)
        out_f[rows] = mm(out_v[rows, :], compress_v[...]).astype(BF16)

    @pl.when(seg > 0)
    def _():
        arr_copy.wait()

    @pl.when(seg < last)
    def _():
        ret_copy.wait()

    @pl.when(seg == last)
    def _():
        seed_copy.wait()

    def replay_section(t):
        section(replay_index(t), lax.rem(t, 2), False)

    @pl.when(seg == 0)
    def _():
        embed_share(0)

    ahead = jnp.where(seg == last, 0, jnp.where(seg == 0, min(2, ticks), 1))

    def early(t, carry):
        replay_section(t)
        return carry

    lax.fori_loop(0, ahead, early, 0)

    def tick(t, carry):
        more = t + 1 < ticks

        @pl.when(seg == 0)
        def _():
            for off in range(1, head_groups):
                theirs = lax.rem(me + head_groups - off, head_groups)
                pltpu.make_async_remote_copy(
                    src_ref=coef.at[t, rows_of(theirs)],
                    dst_ref=coef.at[t, rows_of(theirs)],
                    send_sem=e3_send.at[t, off],
                    recv_sem=e3_recv.at[t, off],
                    device_id={"segment": seg, "head": peer(off)},
                    device_id_type=MESH,
                ).wait_recv()

        @pl.when(jnp.logical_and(seg > 0, t > 0))
        def _():
            for from_head in range(head_groups):
                ag_copy(0, t - 1, from_head, from_head).wait_recv()

        @pl.when(jnp.logical_and(seg > 0, more))
        def _():
            e1_copy(t + 1, seg).start()

        forward(t)

        @pl.when(t > 0)
        def _():
            finish_backward(t - 1)

        @pl.when(jnp.logical_and(seg == 0, more))
        def _():
            embed_sum(t + 1)

        @pl.when(jnp.logical_and(t + 1 >= ahead, jnp.logical_and(seg < last, more)))
        def _():
            replay_section(t + 1)

        @pl.when(jnp.logical_and(seg == 0, more))
        def _():
            embed_share(t + 1)

        finish_forward(t)

        @pl.when(jnp.logical_and(seg < last, t > 0))
        def _():
            for from_head in range(head_groups):
                ag_copy(1, t - 1, from_head, from_head).wait_recv()

        backward(t)
        return carry

    lax.fori_loop(0, ticks, tick, 0)
    finish_backward(ticks - 1)

    def drain(t, carry):
        for off in range(1, head_groups):
            rs_copy(0, t, off).wait_send()
            rs_copy(1, t, off).wait_send()

        @pl.when(seg > 0)
        def _():
            e1_copy(t, seg).wait_send()

        @pl.when(seg == 0)
        def _():
            for off in range(1, head_groups):
                e2_copy(t, off).wait_send()
                e3_copy(t, off).wait_send()

        @pl.when(jnp.logical_and(seg < last, t + 1 < ticks))
        def _():
            for to_head in range(head_groups):
                ag_copy(0, t, me, to_head).wait_send()

        @pl.when(jnp.logical_and(seg > 0, t + 1 < ticks))
        def _():
            for to_head in range(head_groups):
                ag_copy(1, t, me, to_head).wait_send()

        return carry

    lax.fori_loop(0, ticks, drain, 0)


def shards(
    token_ids,
    embed_table,
    arriving,
    returning,
    stashed,
    seed_grad,
    expand,
    compress,
    norm_gain,
    w_query,
    key_weight,
    value_weight,
    w_out,
):
    segments = lax.axis_size("segment")
    head_groups = lax.axis_size("head")
    ticks, span = token_ids.shape
    rank = embed_table.shape[1]
    width = expand.shape[2]
    nq = w_query.shape[2]
    heads = nq // HEAD_SIZE
    share = span // head_groups
    table_rows = embed_table.shape[0]
    vmem = pl.BlockSpec(memory_space=pltpu.VMEM)
    hbm = pl.BlockSpec(memory_space=pl.ANY)
    V = pltpu.VMEM
    D = pltpu.SemaphoreType.DMA
    pieces = nq // min(256, nq)
    all_cols = nq + 2 * HEAD_SIZE
    slots = 4
    out = jax.ShapeDtypeStruct((1, ticks, share, rank), BF16)
    return pl.pallas_call(
        functools.partial(
            relay, segments=segments, head_groups=head_groups, table_rows=table_rows
        ),
        out_shape=(out, out),
        in_specs=[vmem] * 3 + [hbm] * 10,
        out_specs=(vmem, vmem),
        scratch_shapes=[
            V((rank, width), BF16),
            V((width, rank), BF16),
            V((width, nq), BF16),
            V((width, 2 * HEAD_SIZE), BF16),
            V((nq, width), BF16),
            V((rank, all_cols), BF16),
            V((nq, rank), BF16),
            V((2, rank, rank), BF16),
            V((2, rank, rank), BF16),
            V((2 * ticks, span, rank), BF16),
            V((ticks, span, rank), BF16),
            V((slots, span, rank), F32),
            V((slots, span, 1), F32),
            V((slots, heads // 2, 2, span, HEAD_SIZE), BF16),
            V((slots, heads // 2, 2, span, 1), F32),
            V((slots, span, HEAD_SIZE), BF16),
            V((slots, span, 1), F32),
            V((slots, span, HEAD_SIZE), BF16),
            V((slots, heads // 2, 2, span, span), BF16),
            V((span, nq), BF16),
            V((2, span, HEAD_SIZE), F32),
            V((span, all_cols), BF16),
            V((2, ticks, span, rank), BF16),
            V((2, ticks, share, rank), BF16),
            V((2, ticks, head_groups, share, rank), BF16),
            V((ticks, span, rank), BF16),
            V((segments, ticks, span, rank), BF16),
            V((ticks, span, rank), BF16),
            V((ticks, head_groups, share, rank), BF16),
            V((HEAD_SIZE, rank), BF16),
            D((7 + 2 * pieces,)),
            D((2, ticks, head_groups)),
            D((2, ticks, head_groups)),
            D((2, ticks, head_groups)),
            D((2, ticks, head_groups)),
            D((ticks,)),
            D((segments, ticks)),
            D((ticks, head_groups)),
            D((ticks, head_groups)),
            D((ticks, head_groups)),
            D((ticks, head_groups)),
        ],
        compiler_params=pltpu.CompilerParams(
            collective_id=0, has_side_effects=True, vmem_limit_bytes=62 << 20
        ),
        name="relay",
    )(
        token_ids,
        embed_table,
        norm_gain,
        arriving,
        returning,
        stashed,
        seed_grad,
        expand,
        compress,
        w_query,
        key_weight,
        value_weight,
        w_out,
    )


def solution(mesh):
    return jax.shard_map(
        shards,
        mesh=mesh,
        in_specs=(
            P("groups", None),
            P(("segment", "head"), None),
            P(("groups", "segment"), None, None),
            P(("groups", "segment"), None, None),
            P(("groups", "segment"), None, None, None),
            P("groups", None, None),
            P("segment", None, None),
            P("segment", None, None),
            P("segment", None),
            P("segment", None, "head"),
            P("segment", None, None),
            P("segment", None, None),
            P("segment", "head", None),
        ),
        out_specs=(
            P(("groups", "segment"), None, "head", None),
            P(("groups", "segment"), None, "head", None),
        ),
        check_vma=False,
    )
```

```python
import functools
import math

import jax
import jax.numpy as jnp
from jax import lax
from jax.experimental import pallas as pl
from jax.experimental.pallas import tpu as pltpu
from jax.sharding import PartitionSpec as P

QUERY_HEADS = 32
KEY_VALUE_HEADS = 4
HEAD_SIZE = 128
EPS = 1e-06
MESH = pl.DeviceIdType.MESH
F32 = jnp.float32
BF16 = jnp.bfloat16


def mm(former, latter):
    return jnp.dot(former, latter, preferred_element_type=F32)


def mm_back(former, latter):
    return lax.dot_general(former, latter, (((1,), (1,)), ((), ())), preferred_element_type=F32)


def mm_down(former, latter):
    return lax.dot_general(former, latter, (((0,), (0,)), ((), ())), preferred_element_type=F32)


def halves(matrix):
    upper = matrix.astype(BF16)
    return upper, (matrix - upper.astype(F32)).astype(BF16)


def relay(
    ids_ref,
    table_ref,
    gain_ref,
    arriving,
    returning,
    stashed,
    seed_grad,
    expand,
    compress,
    w_query,
    key_weight,
    value_weight,
    w_out,
    fwd_ref,
    bwd_ref,
    expand_v,
    compress_v,
    query_v,
    kv_v,
    out_v,
    qkv_f,
    out_f,
    gram,
    basis,
    coef,
    grad_in,
    mixed_s,
    scale_s,
    qhat_s,
    rq_s,
    khat_s,
    rk_s,
    vals_s,
    probs_s,
    wide_s,
    gkv_acc,
    gcat,
    part,
    own,
    rs_in,
    e_part,
    e_in1,
    e_sum,
    e_in2,
    tail,
    ld_sem,
    rs_send,
    rs_recv,
    ag_send,
    ag_recv,
    e1_send,
    e1_recv,
    e2_send,
    e2_recv,
    e3_send,
    e3_recv,
    *,
    segments,
    head_groups,
    table_rows,
):
    seg = lax.axis_index("segment")
    me = lax.axis_index("head")
    last = segments - 1
    ticks, span = ids_ref.shape
    share = span // head_groups
    width = expand_v.shape[1]
    heads = query_v.shape[1] // HEAD_SIZE
    nq = heads * HEAD_SIZE
    kv_group = QUERY_HEADS // KEY_VALUE_HEADS
    first_kv = me * heads // kv_group
    kv_cols = pl.ds(pl.multiple_of(first_kv * HEAD_SIZE, HEAD_SIZE), HEAD_SIZE)
    inv = 1.0 / math.sqrt(HEAD_SIZE)
    own_rows = pl.ds(pl.multiple_of(me * share, share), share)

    def rows_of(head):
        return pl.ds(pl.multiple_of(head * share, share), share)

    def peer(off):
        return lax.rem(me + off, head_groups)

    qchunk = min(256, nq)
    pieces = nq // qchunk
    loads = [
        (expand.at[0], expand_v),
        *[
            (
                w_query.at[0, :, i * qchunk : (i + 1) * qchunk],
                query_v.at[:, i * qchunk : (i + 1) * qchunk],
            )
            for i in range(pieces)
        ],
        (key_weight.at[0, :, kv_cols], kv_v.at[:, :HEAD_SIZE]),
        (value_weight.at[0, :, kv_cols], kv_v.at[:, HEAD_SIZE:]),
        (stashed.at[0], coef.at[ticks : 2 * ticks]),
        (compress.at[0], compress_v),
        *[
            (
                w_out.at[0, i * qchunk : (i + 1) * qchunk, :],
                out_v.at[i * qchunk : (i + 1) * qchunk, :],
            )
            for i in range(pieces)
        ],
    ]
    loads = [
        pltpu.make_async_copy(src, dst, ld_sem.at[i]) for i, (src, dst) in enumerate(loads)
    ]
    fixed = len(loads)
    arr_copy = pltpu.make_async_copy(arriving.at[0], coef.at[0], ld_sem.at[fixed])
    ret_copy = pltpu.make_async_copy(returning.at[0], grad_in.at[0], ld_sem.at[fixed + 1])
    seed_copy = pltpu.make_async_copy(seed_grad, grad_in, ld_sem.at[fixed + 1])
    for one in loads:
        one.start()

    @pl.when(seg > 0)
    def _():
        arr_copy.start()

    @pl.when(seg < last)
    def _():
        ret_copy.start()

    @pl.when(seg == last)
    def _():
        seed_copy.start()

    barrier = pltpu.get_barrier_semaphore()
    total = segments * head_groups
    mine = seg * head_groups + me
    for off in range(1, total):
        other = lax.rem(mine + off, total)
        pl.semaphore_signal(
            barrier,
            inc=1,
            device_id={
                "segment": other // head_groups,
                "head": lax.rem(other, head_groups),
            },
            device_id_type=MESH,
        )

    base = mine * table_rows
    main = table_rows // HEAD_SIZE * HEAD_SIZE
    rest = table_rows - main
    even = rest // 16 * 16
    tail[...] = jnp.zeros_like(tail)
    if even:
        tail[:even] = table_ref[main : main + even, :]
    if rest > even:
        tail[even:rest] = table_ref[main + even : table_rows, :]

    def pick(t):
        wanted = ids_ref[t : t + 1, :] - base

        def hot(start, count):
            places = lax.broadcasted_iota(jnp.int32, (count, span), 0) + start
            return jnp.where(places == wanted, 1.0, 0.0).astype(BF16)

        rows = mm_down(hot(main, HEAD_SIZE), tail[...])
        if main:
            rows = rows + mm_down(hot(0, main), table_ref[:main, :])
        e_part[t] = rows.astype(BF16)

    pick(0)
    pl.semaphore_wait(barrier, total - 1)

    def e1_copy(t, slot):
        return pltpu.make_async_remote_copy(
            src_ref=e_part.at[t],
            dst_ref=e_in1.at[slot, t],
            send_sem=e1_send.at[t],
            recv_sem=e1_recv.at[slot, t],
            device_id={"segment": 0, "head": me},
            device_id_type=MESH,
        )

    @pl.when(seg > 0)
    def _():
        e1_copy(0, seg).start()

    for t in range(1, ticks):
        pick(t)

    def e2_copy(t, off):
        return pltpu.make_async_remote_copy(
            src_ref=e_sum.at[t, rows_of(peer(off))],
            dst_ref=e_in2.at[t, off],
            send_sem=e2_send.at[t, off],
            recv_sem=e2_recv.at[t, off],
            device_id={"segment": seg, "head": peer(off)},
            device_id_type=MESH,
        )

    def e3_copy(t, off):
        return pltpu.make_async_remote_copy(
            src_ref=coef.at[t, own_rows],
            dst_ref=coef.at[t, own_rows],
            send_sem=e3_send.at[t, off],
            recv_sem=e3_recv.at[t, off],
            device_id={"segment": seg, "head": peer(off)},
            device_id_type=MESH,
        )

    def embed_sum(t):
        total_rows = e_part[t].astype(F32)
        for other in range(1, segments):
            e1_copy(t, other).wait_recv()
            total_rows = total_rows + e_in1[other, t].astype(F32)
        e_sum[t] = total_rows.astype(BF16)
        for off in range(1, head_groups):
            e2_copy(t, off).start()

    def embed_share(t):
        rows = e_sum[t, own_rows].astype(F32)
        for off in range(1, head_groups):
            e2_copy(t, off).wait_recv()
            rows = rows + e_in2[t, off].astype(F32)
        coef[t, own_rows] = rows.astype(BF16)
        for off in range(1, head_groups):
            e3_copy(t, off).start()

    def rs_copy(way, t, off):
        return pltpu.make_async_remote_copy(
            src_ref=part.at[way, t, rows_of(peer(off))],
            dst_ref=rs_in.at[way, t, off],
            send_sem=rs_send.at[way, t, off],
            recv_sem=rs_recv.at[way, t, off],
            device_id={"segment": seg, "head": peer(off)},
            device_id_type=MESH,
        )

    def ag_copy(way, t, from_head, to_head):
        target = coef if way == 0 else grad_in
        return pltpu.make_async_remote_copy(
            src_ref=own.at[way, t],
            dst_ref=target.at[t + 1, rows_of(from_head)],
            send_sem=ag_send.at[way, t, to_head],
            recv_sem=ag_recv.at[way, t, from_head],
            device_id={"segment": seg + (1 if way == 0 else -1), "head": to_head},
            device_id_type=MESH,
        )

    def summed(way, t):
        rows = part[way, t, own_rows].astype(F32)
        for off in range(1, head_groups):
            rs_copy(way, t, off).wait_recv()
            rows = rows + rs_in[way, t, off].astype(F32)
        return rows

    def pass_on(way, t):
        for to_head in range(head_groups):
            ag_copy(way, t, me, to_head).start()

    def replay_index(t):
        source = t - 2 * (last - seg)
        return jnp.where(source >= 0, source, ticks + t)

    def state_slot(t):
        return jnp.where(seg == last, 2 + lax.rem(t, 2), lax.rem(t, 2))

    half = span // 2

    def pair_cols(i):
        return pl.ds(pl.multiple_of(i * 2 * HEAD_SIZE, 2 * HEAD_SIZE), 2 * HEAD_SIZE)

    causal = []
    for rb in range(2):
        shape = (half, (rb + 1) * half)
        row = lax.broadcasted_iota(jnp.int32, shape, 0) + rb * half
        row = jnp.concatenate([row, row], axis=0)
        causal.append(lax.broadcasted_iota(jnp.int32, row.shape, 1) <= row)

    def section(index, slot, with_out):
        c = coef[index]
        wide = c.astype(F32)
        mixed = mm(c, gram[0]) + mm(c, gram[1])
        scaling = lax.rsqrt(jnp.sum(mixed * wide, axis=-1, keepdims=True) / width + EPS)
        mixed_s[slot] = mixed
        scale_s[slot] = scaling
        kv = mm(c, qkv_f[:, nq:]) * scaling
        keys = kv[:, :HEAD_SIZE]
        rk = lax.rsqrt(jnp.mean(keys * keys, axis=-1, keepdims=True) + EPS)
        khat = (keys * rk).astype(BF16)
        values = kv[:, HEAD_SIZE:].astype(BF16)
        khat_s[slot] = khat
        rk_s[slot] = rk
        vals_s[slot] = values

        def pair(i, carry):
            cols = pair_cols(i)
            both = mm(coef[index], qkv_f[:, cols]) * scale_s[slot]
            hats = []
            scales = []
            for e in range(2):
                q = both[:, e * HEAD_SIZE : (e + 1) * HEAD_SIZE]
                rq = lax.rsqrt(jnp.mean(q * q, axis=-1, keepdims=True) + EPS)
                hats.append((q * rq).astype(BF16))
                scales.append(rq)
            for rb in range(2):
                rows = slice(rb * half, (rb + 1) * half)
                known = (rb + 1) * half
                qq = jnp.concatenate([x[rows] for x in hats], axis=0)
                qhat_s[slot, i, rb] = qq
                rq_s[slot, i, rb] = jnp.concatenate([x[rows] for x in scales], axis=0)
                raw = mm_back(qq, khat_s[slot, :known]) * inv
                weights = jnp.where(causal[rb], jnp.exp(raw), 0.0)
                low = (weights * (1.0 / jnp.sum(weights, axis=-1, keepdims=True))).astype(BF16)
                probs_s[slot, i, rb, :, :known] = low
                if with_out:
                    att = mm(low, vals_s[slot, :known]).astype(BF16)
                    wide_s[rows, cols] = jnp.concatenate([att[:half], att[half:]], axis=1)
            return carry

        lax.fori_loop(0, heads // 2, pair, 0)

    def forward(t):
        section(t, 2 + lax.rem(t, 2), True)
        part[0, t] = mm(wide_s[...], out_f[...]).astype(BF16)
        for off in range(1, head_groups):
            rs_copy(0, t, off).start()

    def finish_forward(t):
        c = coef[t, own_rows]
        rows = summed(0, t) + (mm(c, basis[0]) + mm(c, basis[1]))
        rows = rows.astype(BF16)
        own[0, t] = rows
        fwd_ref[0, t] = rows

        @pl.when(jnp.logical_and(seg < last, t + 1 < ticks))
        def _():
            pass_on(0, t)

    def backward(t):
        slot = state_slot(t)
        wide_s[...] = mm_back(grad_in[t], out_f[...]).astype(BF16)
        gkv_acc[...] = jnp.zeros_like(gkv_acc)

        def pair(i, carry):
            cols = pair_cols(i)
            for rb in range(2):
                rows = slice(rb * half, (rb + 1) * half)
                known = (rb + 1) * half
                both = wide_s[rows, cols]
                ga = jnp.concatenate([both[:, :HEAD_SIZE], both[:, HEAD_SIZE:]], axis=0)
                low = probs_s[slot, i, rb, :, :known]
                probs = low.astype(F32)
                gp = mm_back(ga, vals_s[slot, :known])
                inner = jnp.sum(gp * probs, axis=-1, keepdims=True)
                gs = (probs * ((gp - inner) * inv)).astype(BF16)
                qhat = qhat_s[slot, i, rb]
                gqh = mm(gs, khat_s[slot, :known])
                gkv_acc[0, :known] += mm_down(gs, qhat)
                gkv_acc[1, :known] += mm_down(low, ga)
                qw = qhat.astype(F32)
                along = jnp.mean(gqh * qw, axis=-1, keepdims=True)
                gq = (rq_s[slot, i, rb] * (gqh - qw * along)).astype(BF16)
                gcat[rows, cols] = jnp.concatenate([gq[:half], gq[half:]], axis=1)
            return carry

        lax.fori_loop(0, heads // 2, pair, 0)
        gkh = gkv_acc[0]
        kw = khat_s[slot].astype(F32)
        along = jnp.mean(gkh * kw, axis=-1, keepdims=True)
        gcat[:, nq : nq + HEAD_SIZE] = (rk_s[slot] * (gkh - kw * along)).astype(BF16)
        gcat[:, nq + HEAD_SIZE :] = gkv_acc[1].astype(BF16)
        part[1, t] = mm_back(gcat[...], qkv_f[...]).astype(BF16)
        for off in range(1, head_groups):
            rs_copy(1, t, off).start()

    def finish_backward(t):
        slot = state_slot(t)
        c = coef[replay_index(t), own_rows].astype(F32)
        g = grad_in[t, own_rows]
        scaling = scale_s[slot, own_rows]
        pulled = summed(1, t)
        along = jnp.sum(pulled * c, axis=-1, keepdims=True) / width
        direct = mm_back(g, basis[0]) + mm_back(g, basis[1])
        rows = (
            scaling * pulled
            - mixed_s[slot, own_rows] * (scaling * scaling * scaling * along)
            + direct
        ).astype(BF16)
        own[1, t] = rows
        bwd_ref[0, t] = rows

        @pl.when(jnp.logical_and(seg > 0, t + 1 < ticks))
        def _():
            pass_on(1, t)

    loads[0].wait()
    gained = (expand_v[...].astype(F32) * gain_ref[...]).astype(BF16)
    up, low = halves(mm_back(expand_v[...], expand_v[...]))
    gram[0] = up
    gram[1] = low
    for i in range(pieces):
        loads[1 + i].wait()
        cols = slice(i * qchunk, (i + 1) * qchunk)
        qkv_f[:, cols] = mm(gained, query_v[:, cols]).astype(BF16)
    loads[1 + pieces].wait()
    loads[2 + pieces].wait()
    qkv_f[:, nq:] = mm(gained, kv_v[...]).astype(BF16)

    @pl.when(seg == 0)
    def _():
        embed_sum(0)

    loads[3 + pieces].wait()
    loads[4 + pieces].wait()
    up, low = halves(mm(expand_v[...], compress_v[...]))
    basis[0] = up
    basis[1] = low
    for i in range(pieces):
        loads[5 + pieces + i].wait()
        rows = slice(i * qchunk, (i + 1) * qchunk)
        out_f[rows] = mm(out_v[rows, :], compress_v[...]).astype(BF16)

    @pl.when(seg > 0)
    def _():
        arr_copy.wait()

    @pl.when(seg < last)
    def _():
        ret_copy.wait()

    @pl.when(seg == last)
    def _():
        seed_copy.wait()

    def replay_section(t):
        section(replay_index(t), lax.rem(t, 2), False)

    ahead = jnp.where(seg == last, 0, jnp.where(seg == 0, min(2, ticks), 1))

    def early(t, carry):
        replay_section(t)

        @pl.when(jnp.logical_and(seg == 0, t == 0))
        def _():
            embed_share(0)

        return carry

    lax.fori_loop(0, ahead, early, 0)

    def tick(t, carry):
        more = t + 1 < ticks

        @pl.when(seg == 0)
        def _():
            for off in range(1, head_groups):
                theirs = lax.rem(me + head_groups - off, head_groups)
                pltpu.make_async_remote_copy(
                    src_ref=coef.at[t, rows_of(theirs)],
                    dst_ref=coef.at[t, rows_of(theirs)],
                    send_sem=e3_send.at[t, off],
                    recv_sem=e3_recv.at[t, off],
                    device_id={"segment": seg, "head": peer(off)},
                    device_id_type=MESH,
                ).wait_recv()

        @pl.when(jnp.logical_and(seg > 0, t > 0))
        def _():
            for from_head in range(head_groups):
                ag_copy(0, t - 1, from_head, from_head).wait_recv()

        @pl.when(jnp.logical_and(seg > 0, more))
        def _():
            e1_copy(t + 1, seg).start()

        forward(t)

        @pl.when(t > 0)
        def _():
            finish_backward(t - 1)

        @pl.when(jnp.logical_and(seg == 0, more))
        def _():
            embed_sum(t + 1)

        @pl.when(jnp.logical_and(t + 1 >= ahead, jnp.logical_and(seg < last, more)))
        def _():
            replay_section(t + 1)

        @pl.when(jnp.logical_and(seg == 0, more))
        def _():
            embed_share(t + 1)

        finish_forward(t)

        @pl.when(jnp.logical_and(seg < last, t > 0))
        def _():
            for from_head in range(head_groups):
                ag_copy(1, t - 1, from_head, from_head).wait_recv()

        backward(t)
        return carry

    lax.fori_loop(0, ticks, tick, 0)
    finish_backward(ticks - 1)

    def drain(t, carry):
        for off in range(1, head_groups):
            rs_copy(0, t, off).wait_send()
            rs_copy(1, t, off).wait_send()

        @pl.when(seg > 0)
        def _():
            e1_copy(t, seg).wait_send()

        @pl.when(seg == 0)
        def _():
            for off in range(1, head_groups):
                e2_copy(t, off).wait_send()
                e3_copy(t, off).wait_send()

        @pl.when(jnp.logical_and(seg < last, t + 1 < ticks))
        def _():
            for to_head in range(head_groups):
                ag_copy(0, t, me, to_head).wait_send()

        @pl.when(jnp.logical_and(seg > 0, t + 1 < ticks))
        def _():
            for to_head in range(head_groups):
                ag_copy(1, t, me, to_head).wait_send()

        return carry

    lax.fori_loop(0, ticks, drain, 0)


def shards(
    token_ids,
    embed_table,
    arriving,
    returning,
    stashed,
    seed_grad,
    expand,
    compress,
    norm_gain,
    w_query,
    key_weight,
    value_weight,
    w_out,
):
    segments = lax.axis_size("segment")
    head_groups = lax.axis_size("head")
    ticks, span = token_ids.shape
    rank = embed_table.shape[1]
    width = expand.shape[2]
    nq = w_query.shape[2]
    heads = nq // HEAD_SIZE
    share = span // head_groups
    table_rows = embed_table.shape[0]
    vmem = pl.BlockSpec(memory_space=pltpu.VMEM)
    hbm = pl.BlockSpec(memory_space=pl.ANY)
    V = pltpu.VMEM
    D = pltpu.SemaphoreType.DMA
    pieces = nq // min(256, nq)
    all_cols = nq + 2 * HEAD_SIZE
    slots = 4
    out = jax.ShapeDtypeStruct((1, ticks, share, rank), BF16)
    return pl.pallas_call(
        functools.partial(
            relay, segments=segments, head_groups=head_groups, table_rows=table_rows
        ),
        out_shape=(out, out),
        in_specs=[vmem] * 3 + [hbm] * 10,
        out_specs=(vmem, vmem),
        scratch_shapes=[
            V((rank, width), BF16),
            V((width, rank), BF16),
            V((width, nq), BF16),
            V((width, 2 * HEAD_SIZE), BF16),
            V((nq, width), BF16),
            V((rank, all_cols), BF16),
            V((nq, rank), BF16),
            V((2, rank, rank), BF16),
            V((2, rank, rank), BF16),
            V((2 * ticks, span, rank), BF16),
            V((ticks, span, rank), BF16),
            V((slots, span, rank), F32),
            V((slots, span, 1), F32),
            V((slots, heads // 2, 2, span, HEAD_SIZE), BF16),
            V((slots, heads // 2, 2, span, 1), F32),
            V((slots, span, HEAD_SIZE), BF16),
            V((slots, span, 1), F32),
            V((slots, span, HEAD_SIZE), BF16),
            V((slots, heads // 2, 2, span, span), BF16),
            V((span, nq), BF16),
            V((2, span, HEAD_SIZE), F32),
            V((span, all_cols), BF16),
            V((2, ticks, span, rank), BF16),
            V((2, ticks, share, rank), BF16),
            V((2, ticks, head_groups, share, rank), BF16),
            V((ticks, span, rank), BF16),
            V((segments, ticks, span, rank), BF16),
            V((ticks, span, rank), BF16),
            V((ticks, head_groups, share, rank), BF16),
            V((HEAD_SIZE, rank), BF16),
            D((7 + 2 * pieces,)),
            D((2, ticks, head_groups)),
            D((2, ticks, head_groups)),
            D((2, ticks, head_groups)),
            D((2, ticks, head_groups)),
            D((ticks,)),
            D((segments, ticks)),
            D((ticks, head_groups)),
            D((ticks, head_groups)),
            D((ticks, head_groups)),
            D((ticks, head_groups)),
        ],
        compiler_params=pltpu.CompilerParams(
            collective_id=0, has_side_effects=True, vmem_limit_bytes=62 << 20
        ),
        name="relay",
    )(
        token_ids,
        embed_table,
        norm_gain,
        arriving,
        returning,
        stashed,
        seed_grad,
        expand,
        compress,
        w_query,
        key_weight,
        value_weight,
        w_out,
    )


def solution(mesh):
    return jax.shard_map(
        shards,
        mesh=mesh,
        in_specs=(
            P("groups", None),
            P(("segment", "head"), None),
            P(("groups", "segment"), None, None),
            P(("groups", "segment"), None, None),
            P(("groups", "segment"), None, None, None),
            P("groups", None, None),
            P("segment", None, None),
            P("segment", None, None),
            P("segment", None),
            P("segment", None, "head"),
            P("segment", None, None),
            P("segment", None, None),
            P("segment", "head", None),
        ),
        out_specs=(
            P(("groups", "segment"), None, "head", None),
            P(("groups", "segment"), None, "head", None),
        ),
        check_vma=False,
    )
```
